256 devices in a mesh: cube: 4 (over y), row: 4 (over x), col: 16 (over z, core).
Axes of the slice: x: 4, y: 4, z: 8, core: 2. Of those that a mesh axis runs over, the one named last changes fastest.
Arguments:
- front_entries: float32 [4, 8192, 8192], P('cube', 'row', 'col'), as said below
- child_updates: float32 [4, 2, 4096, 4096], P('cube', None, ('row', 'col')), may hold values from -6 to 6, as said below
- child_index: int32 [4, 2, 64], replicated, may hold values from 0 to 127, as said below
- child_blocks: int32 [4, 2], replicated, may hold values from 32 to 64
Outputs:
- factored: float32 [4, 8192, 8192], P('cube', 'row', 'col')
The draws below stay inside these ranges and needn't reach their ends.
Inputs may be any that keep to these rules, and one draw needn't show every extreme that they name: `front_entries`: each front is symmetric positive definite in natural numbering. `child_updates`: each contribution block is symmetric. `child_index`: each list names 64 different front blocks; entry t of a list names a front block whose rows lie in a 512-wide block b of front variables with b mod 4 = t div (16).
All inputs are finite; a program needn't handle non-finite values.
Results may differ from the reference program's by a relative error of at most 0.0001.
Values sent between devices are 32-bit elements; how exact they have to be, the bound alone decides.
No kernel may reach another device: no remote copies, remote signals or barrier semaphores. Data moves between devices by JAX's collectives and lax.ppermute only.
A program may use at most 128 MiB of HBM per device.

```python
import math
import jax
import jax.numpy as jnp
from jax import lax

F = 8192
B = 512
SBLK = 64
CR = 4096
PANELS = 2
NPB = 128
CBLK = 64
N_CUBE = 4
N_ROW = 4
N_COL = 16


def natural_variable_drawn(parts):
    place = jnp.arange(F, dtype=jnp.int32)
    local_size = F // parts
    local = place % local_size
    return (local // B * parts + place // local_size) * B + local % B


def draw_front_entries(key, part):
    row_back = natural_variable_drawn(N_ROW)
    col_back = natural_variable_drawn(N_COL)

    def one_front(subkey):
        first, second, third = jax.random.split(subkey, 3)
        base = jnp.clip(jax.random.normal(first, (F, F), jnp.float32), -6.0, 6.0)
        scales = jax.random.uniform(second, (F,), jnp.float32, 4.0, 8.0)
        weights = jax.random.uniform(third, (F,), jnp.float32, 0.6, 1.6)
        amplitude = 4.0
        symmetric = (base + base.T) * 0.7071
        place = jnp.arange(F, dtype=jnp.float32)
        distance = jnp.abs(place[:, None] - place[None, :])
        coupling = amplitude * weights[:, None] * weights[None, :] * jnp.exp(-distance / (0.5 * B))
        symmetric = symmetric + coupling + jnp.diag(scales * math.sqrt(F))
        return symmetric[row_back][:, col_back]
    return lax.map(one_front, jax.random.split(key, N_CUBE))


def draw_child_updates(key, part):

    def one_child(subkey):
        base = jnp.clip(jax.random.normal(subkey, (CR, CR), jnp.float32), -6.0, 6.0) * 0.7
        return (base + base.T) * 0.7071
    return lax.map(one_child, jax.random.split(key, N_CUBE * 2)).reshape(N_CUBE, 2, CR, CR)


def draw_child_index(key, part):
    group_size = CBLK // N_ROW
    owned_blocks = NPB // N_ROW
    per_panel = B // SBLK

    def one_group(subkey):
        return jax.random.permutation(subkey, owned_blocks)[:group_size].astype(jnp.int32)
    picks = lax.map(one_group, jax.random.split(key, N_CUBE * 2 * N_ROW)).reshape(N_CUBE * 2, N_ROW, group_size)
    first_group = picks[0, 0]
    first_group = first_group.at[0].set(jnp.where(jnp.any(first_group == 0), first_group[0], 0))
    last_group = picks[0, N_ROW - 1]
    last_group = last_group.at[0].set(jnp.where(jnp.any(last_group == owned_blocks - 1), last_group[0], owned_blocks - 1))
    picks = picks.at[0, 0].set(first_group)
    picks = picks.at[0, N_ROW - 1].set(last_group)
    owner = jnp.arange(N_ROW, dtype=jnp.int32)[None, :, None]
    chosen = (picks // per_panel * N_ROW + owner) * per_panel + picks % per_panel
    return chosen.reshape(N_CUBE, 2, CBLK).astype(jnp.int32)


def draw_child_blocks(key, part):
    counts = jax.random.randint(key, (N_CUBE * 2,), CBLK // 2, CBLK + 1, dtype=jnp.int32)
    chosen = jax.random.randint(jax.random.fold_in(key, 3), (), 0, N_CUBE * 2, dtype=jnp.int32)
    counts = jnp.where(jnp.arange(N_CUBE * 2, dtype=jnp.int32) == chosen, CBLK, counts)
    return counts.reshape(N_CUBE, 2).astype(jnp.int32)


def setup_inputs(seed: int = 0) -> dict:
    keys = jax.random.split(jax.random.key(seed), 5)
    front_entries = draw_front_entries(jax.random.fold_in(keys[4], 71), 0)
    child_updates = draw_child_updates(jax.random.fold_in(keys[4], 71), 0)
    child_index = draw_child_index(jax.random.fold_in(keys[4], 71), 0)
    child_blocks = draw_child_blocks(jax.random.fold_in(keys[4], 71), 0)
    return {"front_entries": front_entries, "child_updates": child_updates, "child_index": child_index, "child_blocks": child_blocks}


HIGHEST_PRECISION = lax.Precision.HIGHEST

def storage_position(variable, parts):
    local_size = F // parts
    block = variable // B
    return block % parts * local_size + block // parts * B + variable % B

def natural_variable(parts):
    place = jnp.arange(F, dtype=jnp.int32)
    local_size = F // parts
    local = place % local_size
    return (local // B * parts + place // local_size) * B + local % B

def reference(front_entries, child_updates, child_index, child_blocks):
    natural = jnp.arange(F, dtype=jnp.int32)
    row_place = storage_position(natural, N_ROW)
    col_place = storage_position(natural, N_COL)
    row_back = natural_variable(N_ROW)
    col_back = natural_variable(N_COL)
    blocks = natural // B
    offsets = jnp.arange(CR, dtype=jnp.int32)
    results = []
    for front_number in range(N_CUBE):
        matrix = front_entries[front_number][row_place][:, col_place]
        for child_slot, source in ((0, front_number), (1, front_number ^ 1)):
            live_mask = offsets // SBLK < child_blocks[source, child_slot]
            variables = child_index[source, child_slot][offsets // SBLK] * SBLK + offsets % SBLK
            values = jnp.where(live_mask[:, None] & live_mask[None, :], child_updates[source, child_slot], 0.0)
            matrix = matrix.at[variables[:, None], variables[None, :]].add(values)
        for panel_step in range(PANELS):
            first_row = panel_step * B
            factor = jnp.linalg.cholesky(matrix[first_row:first_row + B, first_row:first_row + B])
            solved = lax.linalg.triangular_solve(factor, matrix[:, first_row:first_row + B], left_side=False, lower=True, transpose_a=True)
            solved = jnp.where((blocks < panel_step)[:, None], 0.0, solved)
            solved = solved.at[first_row:first_row + B].set(factor)
            matrix = matrix - jnp.dot(solved.astype(jnp.float32), solved.T.astype(jnp.float32), precision=HIGHEST_PRECISION, preferred_element_type=jnp.float32)
            matrix = matrix.at[:, first_row:first_row + B].set(solved)
        finished = (blocks < PANELS)[:, None] & (blocks >= PANELS)[None, :]
        matrix = jnp.where(finished, 0.0, matrix)
        results.append(matrix[row_back][:, col_back])
    return jnp.stack(results)
```

```python
import jax
import jax.numpy as jnp
from jax import lax
from jax.experimental import pallas as pl
from jax.experimental.pallas import tpu as pltpu
from jax.sharding import PartitionSpec as P

F = 8192
B = 512
SBLK = 64
CR = 4096
PANELS = 2
PIVOTS = PANELS * B
PER_PANEL = B // SBLK
TILE = 128
HIGHEST = lax.Precision.HIGHEST
VMEM = pltpu.VMEM
SMEM = pltpu.SMEM


def vmem_spec():
    return pl.BlockSpec(memory_space=VMEM)


def smem_spec():
    return pl.BlockSpec(memory_space=SMEM)


def widen_kernel(list_ref, live_ref, rows_ref, out_ref):
    out_ref[...] = jnp.zeros_like(out_ref)
    lane = lax.broadcasted_iota(jnp.int32, (SBLK, TILE), 1)

    def place(pair, carry):
        both = rows_ref[:, pl.ds(pl.multiple_of(pair * TILE, TILE), TILE)]
        other = pltpu.roll(both, SBLK, 1)
        for half in range(2):
            block = pair * 2 + half
            target = list_ref[block]
            parity = target % 2
            offset = pl.multiple_of(target % PER_PANEL // 2 * TILE, TILE)
            owner = target // PER_PANEL
            moved = jnp.where(parity == half, both, other)
            keep = (lane // SBLK == parity) & (block < live_ref[0])
            spot = (owner, slice(None), pl.ds(offset, TILE))
            out_ref[spot] = jnp.where(keep, moved, out_ref[spot])
        return carry

    lax.fori_loop(0, CR // TILE, place, 0)


def widen(blocks, live, rows):
    return pl.pallas_call(
        widen_kernel,
        out_shape=jax.ShapeDtypeStruct((F // B, SBLK, B), jnp.float32),
        in_specs=[smem_spec(), smem_spec(), vmem_spec()],
        out_specs=vmem_spec(),
        compiler_params=pltpu.CompilerParams(vmem_limit_bytes=16 << 20),
        name="widen",
    )(blocks, live, rows)


def pivot_part_kernel(place_ref, first_ref, second_ref, corner_ref, out_ref):
    out_ref[...] = jnp.zeros_like(out_ref)
    row_index, col_index = place_ref[2], place_ref[3]

    @pl.when((row_index < PANELS) & (col_index < PANELS))
    def _():
        rows = pl.ds(pl.multiple_of(row_index * B, B), B)
        cols = pl.ds(pl.multiple_of(col_index * B, B), B)
        out_ref[rows, cols] = corner_ref[...]

    for child, source in enumerate((first_ref, second_ref)):
        target = place_ref[child]

        @pl.when(target < PANELS * PER_PANEL)
        def _():
            rows = pl.ds(pl.multiple_of(target * SBLK, SBLK), SBLK)
            for panel in range(PANELS):
                cols = slice(panel * B, panel * B + B)
                out_ref[rows, cols] = out_ref[rows, cols] + source[panel]


def pivot_part(place, first, second, corner):
    return pl.pallas_call(
        pivot_part_kernel,
        out_shape=jax.ShapeDtypeStruct((PIVOTS, PIVOTS), jnp.float32),
        in_specs=[smem_spec()] + [vmem_spec()] * 3,
        out_specs=vmem_spec(),
        compiler_params=pltpu.CompilerParams(vmem_limit_bytes=16 << 20),
        name="pivot_part",
    )(place, first, second, corner)


def factor_tile(tile):
    count = TILE // 8
    groups = [tile[8 * g : 8 * g + 8, :] for g in range(count)]
    lane = lax.broadcasted_iota(jnp.int32, (8, TILE), 1)
    sub = lax.broadcasted_iota(jnp.int32, (8, TILE), 0)
    for j in range(TILE):
        g, q = divmod(j, 8)
        at_j = lane == j
        cols = [jnp.broadcast_to(groups[i][:, j : j + 1], (8, TILE)) for i in range(g, count)]
        recip = 1.0 / jnp.broadcast_to(cols[0][q : q + 1, :], (8, TILE))
        row = jnp.broadcast_to(groups[g][q : q + 1, :], (8, TILE)) * recip
        row = jnp.where(at_j, recip, row)
        below = sub > q
        groups[g] = jnp.where(at_j & below, 0.0, groups[g]) - jnp.where(below, cols[0], 0.0) * row
        for i in range(g + 1, count):
            groups[i] = jnp.where(at_j, 0.0, groups[i]) - cols[i - g] * row
    return jnp.concatenate(groups, axis=0)


def inverse_factor_tile(tile):
    out = factor_tile(tile)
    lane = lax.broadcasted_iota(jnp.int32, (TILE, TILE), 1)
    sub = lax.broadcasted_iota(jnp.int32, (TILE, TILE), 0)
    pivots = jnp.sum(jnp.where(lane == sub, out, 0.0), axis=1, keepdims=True)
    root = lax.rsqrt(pivots)
    root = root * (1.5 - 0.5 * pivots * root * root)
    return jnp.where(lane < sub, out, jnp.where(lane == sub, 1.0, 0.0)) * root


def inverse_factor_kernel(square_ref, inv_ref, row_ref):
    inv_ref[...] = square_ref[...]
    lane = lax.broadcasted_iota(jnp.int32, (TILE, TILE), 1)
    sub = lax.broadcasted_iota(jnp.int32, (TILE, TILE), 0)
    identity = jnp.where(lane == sub, 1.0, 0.0)
    steps = PIVOTS // TILE

    def step(k, carry):
        at = pl.ds(pl.multiple_of(k * TILE, TILE), TILE)
        inv_tile = inverse_factor_tile(inv_ref[at, at])
        inv_ref[at, at] = identity
        row_ref[...] = jnp.dot(
            inv_tile, inv_ref[at, :], precision=HIGHEST, preferred_element_type=jnp.float32
        )
        inv_ref[at, :] = row_ref[...]

        def below(i, carry):
            rows = pl.ds(pl.multiple_of(i * TILE, TILE), TILE)
            left = row_ref[:, rows]
            inv_ref[rows, at] = jnp.zeros((TILE, TILE), jnp.float32)
            inv_ref[rows, :] = inv_ref[rows, :] - lax.dot_general(
                left,
                row_ref[...],
                (((0,), (0,)), ((), ())),
                precision=HIGHEST,
                preferred_element_type=jnp.float32,
            )
            return carry

        return lax.fori_loop(k + 1, steps, below, carry)

    lax.fori_loop(0, steps, step, 0)
    for k in range(steps - 1):
        rows = slice(k * TILE, k * TILE + TILE)
        inv_ref[rows, (k + 1) * TILE :] = jnp.zeros((TILE, PIVOTS - (k + 1) * TILE), jnp.float32)


def inverse_factor(square):
    return pl.pallas_call(
        inverse_factor_kernel,
        out_shape=jax.ShapeDtypeStruct((PIVOTS, PIVOTS), jnp.float32),
        in_specs=[vmem_spec()],
        out_specs=vmem_spec(),
        scratch_shapes=[pltpu.VMEM((TILE, PIVOTS), jnp.float32)],
        compiler_params=pltpu.CompilerParams(vmem_limit_bytes=32 << 20),
        name="inverse_factor",
    )(square)


def top_rows_kernel(target_ref, front_ref, first_ref, second_ref, out_ref):
    out_ref[...] = front_ref[...]
    for child, source in enumerate((first_ref, second_ref)):
        for t in range(source.shape[0]):
            target = target_ref[child, t]

            @pl.when(target // (PER_PANEL * 4) == 0)
            def _():
                rows = pl.ds(pl.multiple_of(target % PER_PANEL * SBLK, SBLK), SBLK)
                out_ref[rows, :] = out_ref[rows, :] + source[t]


def top_rows(targets, front, first, second):
    return pl.pallas_call(
        top_rows_kernel,
        grid=(1,),
        out_shape=jax.ShapeDtypeStruct((B, B), jnp.float32),
        in_specs=[
            smem_spec(),
            pl.BlockSpec((B, B), lambda i: (0, 0)),
            vmem_spec(),
            vmem_spec(),
        ],
        out_specs=pl.BlockSpec((B, B), lambda i: (0, 0)),
        compiler_params=pltpu.CompilerParams(vmem_limit_bytes=24 << 20),
        name="top_rows",
    )(targets, front, first, second)


def finish_kernel(
    target_ref, place_ref, front_ref, first_ref, second_ref, base_ref, extra_ref, right_ref,
    out_ref, left_ref,
):
    slot = pl.program_id(0)
    row_index, col_index = place_ref[2], place_ref[3]
    pieces = base_ref.shape[0]
    width = base_ref.shape[2]
    for piece in range(pieces):
        left_ref[:, piece * width : (piece + 1) * width] = base_ref[piece]
    trailing = col_index >= PANELS
    out_ref[...] = jnp.where(trailing, front_ref[...], 0.0)
    for child, source in enumerate((first_ref, second_ref)):
        for t in range(source.shape[0]):
            target = target_ref[child, t]

            @pl.when(target // (PER_PANEL * 4) == slot)
            def _():
                rows = pl.ds(pl.multiple_of(target % PER_PANEL * SBLK, SBLK), SBLK)
                left_ref[rows, :] = left_ref[rows, :] + extra_ref[t, child * SBLK : (child + 1) * SBLK, :]

                @pl.when(trailing)
                def _():
                    out_ref[rows, :] = out_ref[rows, :] + source[t]

    total = out_ref[...] + jnp.dot(
        left_ref[...], right_ref[...], precision=HIGHEST, preferred_element_type=jnp.float32
    )
    block = slot * 4 + row_index
    row = block * B + lax.broadcasted_iota(jnp.int32, (B, B), 0)
    col = col_index * B + lax.broadcasted_iota(jnp.int32, (B, B), 1)
    upper = (row < PIVOTS) & (row < col)
    out_ref[...] = jnp.where(upper, 0.0, total)


def finish(targets, place, front, first, second, base, extra, right):
    slots = front.shape[0] // B
    pieces = base.shape[0] // slots
    return pl.pallas_call(
        finish_kernel,
        grid=(slots,),
        out_shape=jax.ShapeDtypeStruct(front.shape, jnp.float32),
        in_specs=[
            smem_spec(),
            smem_spec(),
            pl.BlockSpec((B, B), lambda s: (s, 0)),
            vmem_spec(),
            vmem_spec(),
            pl.BlockSpec((pieces,) + base.shape[1:], lambda s: (s, 0, 0)),
            vmem_spec(),
            vmem_spec(),
        ],
        out_specs=pl.BlockSpec((B, B), lambda s: (s, 0)),
        scratch_shapes=[pltpu.VMEM((B, PIVOTS), jnp.float32)],
        compiler_params=pltpu.CompilerParams(vmem_limit_bytes=48 << 20),
        name="finish",
    )(targets, place, front, first, second, base, extra, right)


def exchange(value):
    return lax.all_to_all(value, "col", split_axis=0, concat_axis=0, tiled=True)


def on_device(front_entries, child_updates, child_index, child_blocks):
    n_row = lax.axis_size("row")
    n_col = lax.axis_size("col")
    n_cube = lax.axis_size("cube")
    row_index = lax.axis_index("row")
    col_index = lax.axis_index("col")
    cube_index = lax.axis_index("cube")
    sibling = jnp.bitwise_xor(cube_index, 1)
    front = front_entries[0]
    block_lists = jnp.stack([child_index[cube_index, 0], child_index[sibling, 1]])
    counts = jnp.stack([child_blocks[cube_index, 0], child_blocks[sibling, 1]])
    own_block = row_index * n_col + col_index
    targets = lax.dynamic_slice(block_lists, (0, row_index * n_col), (2, n_col))
    place = jnp.concatenate([block_lists[:, own_block], row_index[None], col_index[None]])
    live = jnp.where(own_block < counts, counts, 0)

    turned = front[:B].T
    half = B // 2
    paths = [[], []]
    for part in range(2):
        for source_row in range(PANELS):
            for block in range(n_col):
                source = source_row * n_col + block
                dest = block % n_row * n_col + block // n_row * n_row + source_row * 2 + part
                paths[part].append((source, dest))
    received = [
        lax.ppermute(turned[:, part * half : (part + 1) * half], ("row", "col"), paths[part])
        for part in range(2)
    ]
    own_piece = jnp.where(col_index % 2 == 0, received[0], received[1])
    base = lax.all_gather(own_piece, "col", axis=0, tiled=False)

    swap = [(cube, cube ^ 1) for cube in range(n_cube)]
    arrived_child = lax.ppermute(child_updates[0, 1], "cube", swap)
    spread_first = widen(block_lists[0], live[0:1], child_updates[0, 0])
    spread_second = widen(block_lists[1], live[1:2], arrived_child)

    part = pivot_part(place, spread_first[:PANELS], spread_second[:PANELS], front[:B])
    square = lax.psum(part, ("row", "col"))
    inverse = inverse_factor(square)

    extra_own = jnp.concatenate(
        [
            jnp.concatenate([spread[panel] for panel in range(PANELS)], axis=1)
            for spread in (spread_first, spread_second)
        ],
        axis=0,
    )
    extra = lax.all_gather(extra_own, "col", axis=0, tiled=False)
    first = exchange(spread_first)
    second = exchange(spread_second)
    top = top_rows(targets, front, first, second)
    tops = lax.all_gather(top, "row", axis=0, tiled=False)
    above = tops[:PANELS].reshape(PIVOTS, B)
    solved = jnp.dot(inverse, above, precision=HIGHEST, preferred_element_type=jnp.float32)
    solved = -jnp.dot(inverse.T, solved, precision=HIGHEST, preferred_element_type=jnp.float32)
    own_cols = lax.dynamic_slice_in_dim(inverse, jnp.minimum(col_index, PANELS - 1) * B, B, 0).T
    right = jnp.where(col_index < PANELS, own_cols, solved)
    return finish(targets, place, front, first, second, base, extra, right)[None]


def solution(mesh):
    in_specs = (P("cube", "row", "col"), P("cube", None, ("row", "col"), None), P(), P())
    out_specs = P("cube", "row", "col")
    return jax.shard_map(
        on_device, mesh=mesh, in_specs=in_specs, out_specs=out_specs, check_vma=False
    )
```

```python
import jax
import jax.numpy as jnp
from jax import lax
from jax.experimental import pallas as pl
from jax.experimental.pallas import tpu as pltpu
from jax.sharding import PartitionSpec as P

F = 8192
B = 512
SBLK = 64
CR = 4096
PANELS = 2
PIVOTS = PANELS * B
PER_PANEL = B // SBLK
TILE = 128
GROUP = 8
HIGHEST = lax.Precision.HIGHEST
VMEM = pltpu.VMEM
SMEM = pltpu.SMEM


def vmem_spec():
    return pl.BlockSpec(memory_space=VMEM)


def smem_spec():
    return pl.BlockSpec(memory_space=SMEM)


def cost(seconds, moved):
    return pl.CostEstimate(flops=int(seconds * 1e15), bytes_accessed=moved, transcendentals=0)


def widen_kernel(list_ref, live_ref, first_ref, second_ref, out_ref):
    out_ref[...] = jnp.zeros_like(out_ref)
    lane = lax.broadcasted_iota(jnp.int32, (SBLK, TILE), 1)
    for child, rows_ref in enumerate((first_ref, second_ref)):
        out_rows = slice(child * SBLK, (child + 1) * SBLK)

        def place(pair, carry):
            both = rows_ref[:, pl.ds(pl.multiple_of(pair * TILE, TILE), TILE)]
            other = pltpu.roll(both, SBLK, 1)
            for half in range(2):
                block = pair * 2 + half
                target = list_ref[child, block]
                parity = target % 2
                offset = pl.multiple_of(target % PER_PANEL // 2 * TILE, TILE)
                owner = target // PER_PANEL
                moved = jnp.where(parity == half, both, other)
                keep = (lane // SBLK == parity) & (block < live_ref[child])
                spot = (owner, out_rows, pl.ds(offset, TILE))
                out_ref[spot] = jnp.where(keep, moved, out_ref[spot])
            return carry

        lax.fori_loop(0, CR // TILE, place, 0)


def widen(lists, live, first, second):
    return pl.pallas_call(
        widen_kernel,
        out_shape=jax.ShapeDtypeStruct((F // B, 2 * SBLK, B), jnp.float32),
        in_specs=[smem_spec(), smem_spec(), vmem_spec(), vmem_spec()],
        out_specs=vmem_spec(),
        compiler_params=pltpu.CompilerParams(vmem_limit_bytes=16 << 20),
        cost_estimate=cost(8e-6, 6 << 20),
        name="widen",
    )(lists, live, first, second)


def pick_kernel(list_ref, live_ref, rows_ref, first_ref, second_ref):
    lane = lax.broadcasted_iota(jnp.int32, (SBLK, TILE), 1)
    for child, out_ref in enumerate((first_ref, second_ref)):
        out_ref[...] = jnp.zeros_like(out_ref)
        for pair in range(rows_ref.shape[2] // TILE):
            both = rows_ref[child, :, pair * TILE : (pair + 1) * TILE]
            other = pltpu.roll(both, SBLK, 1)
            for half in range(2):
                block = pair * 2 + half
                target = list_ref[child, block]

                @pl.when((target < PANELS * PER_PANEL) & (block < live_ref[child]))
                def _():
                    parity = target % 2
                    moved = jnp.where(parity == half, both, other)
                    spot = pl.ds(pl.multiple_of(target // 2 * TILE, TILE), TILE)
                    out_ref[:, spot] = jnp.where(lane // SBLK == parity, moved, out_ref[:, spot])


def pick(lists, live, rows):
    width = PANELS * CR // 4
    return pl.pallas_call(
        pick_kernel,
        grid=(1,),
        out_shape=[jax.ShapeDtypeStruct((SBLK, PIVOTS), jnp.float32)] * 2,
        in_specs=[smem_spec(), smem_spec(), pl.BlockSpec((2, SBLK, width), lambda i: (0, 0, 0))],
        out_specs=[pl.BlockSpec((SBLK, PIVOTS), lambda i: (0, 0))] * 2,
        compiler_params=pltpu.CompilerParams(vmem_limit_bytes=16 << 20),
        cost_estimate=cost(3e-6, 2 << 20),
        name="pick",
    )(lists, live, rows)


def pivot_block(owner):
    return owner % PANELS * PER_PANEL + owner // PANELS


def turn_kernel(first_ref, second_ref, out_ref):
    half = SBLK // 2
    for child, source in enumerate((first_ref, second_ref)):
        turned = source[...].T
        for owner in range(out_ref.shape[0]):
            at = pivot_block(owner) * SBLK
            out_ref[owner, child] = jnp.concatenate(
                [turned[at : at + half], turned[at + half : at + SBLK]], axis=1
            )


def turn(first, second):
    owners = PIVOTS // SBLK
    return pl.pallas_call(
        turn_kernel,
        out_shape=jax.ShapeDtypeStruct((owners, 2, SBLK // 2, 2 * SBLK), jnp.float32),
        in_specs=[vmem_spec()] * 2,
        out_specs=vmem_spec(),
        cost_estimate=cost(2e-6, 1 << 20),
        name="turn",
    )(first, second)


def chunk_kernel(target_ref, place_ref, *refs):
    base_refs, first_ref, second_ref, out_ref = refs[:-3], refs[-3], refs[-2], refs[-1]
    steps = len(base_refs)
    half = SBLK // 2
    own_piece = place_ref[1] // PANELS
    for slot in range(out_ref.shape[1] // B):
        for step in range(steps):

            @pl.when((step + 2 * slot) % steps == own_piece)
            def _():
                out_ref[:, slot * B : (slot + 1) * B] = base_refs[step][...]

    lane = lax.broadcasted_iota(jnp.int32, (half, TILE), 1)
    for child, source in enumerate((first_ref, second_ref)):
        for t in range(source.shape[0]):
            both = source[t]
            other = pltpu.roll(both, SBLK, 1)
            target = target_ref[child, t]
            parity = target % 2
            offset = target // (PER_PANEL * 4) * B + target % PER_PANEL // 2 * TILE
            spot = pl.ds(pl.multiple_of(offset, TILE), TILE)
            keep = lane // SBLK == parity
            for part in range(2):
                rows = slice(part * half, (part + 1) * half)
                moved = jnp.where(parity == part, both, other)
                out_ref[rows, spot] = out_ref[rows, spot] + jnp.where(keep, moved, 0.0)


def chunk(targets, place, base, first, second, width):
    return pl.pallas_call(
        chunk_kernel,
        out_shape=jax.ShapeDtypeStruct((SBLK, width), jnp.float32),
        in_specs=[smem_spec(), smem_spec()] + [vmem_spec()] * (len(base) + 2),
        out_specs=vmem_spec(),
        cost_estimate=cost(3e-6, 2 << 20),
        name="chunk",
    )(targets, place, *base, first, second)


def spread_over(value):
    return jnp.broadcast_to(value, (GROUP, TILE))


def inverse_factor_tile(tile):
    count = TILE // GROUP
    groups = [tile[GROUP * g : GROUP * g + GROUP, :] for g in range(count)]
    lane = lax.broadcasted_iota(jnp.int32, (GROUP, TILE), 1)
    sub = lax.broadcasted_iota(jnp.int32, (GROUP, TILE), 0)
    done = []
    for g in range(count):
        first = GROUP * g
        here = lane // GROUP == g
        own = groups[g]
        cols = [
            [spread_over(groups[i][:, first + q : first + q + 1]) for q in range(GROUP)]
            for i in range(g, count)
        ]
        square = [
            [spread_over(cols[0][q][i : i + 1, :]) if i >= q else None for q in range(GROUP)]
            for i in range(GROUP)
        ]
        rows = [
            jnp.where(here, jnp.where(lane == first + q, 1.0, 0.0), spread_over(own[q : q + 1, :]))
            for q in range(GROUP)
        ]
        ratio = [[None] * GROUP for _ in range(GROUP)]
        recip = [None] * GROUP
        result = None
        for q in range(GROUP):
            pivot = square[q][q]
            recip[q] = 1.0 / pivot
            for i in range(q + 1, GROUP):
                ratio[i][q] = square[i][q] * recip[q]
            for i in range(q + 1, GROUP):
                for j in range(q + 1, i + 1):
                    square[i][j] = square[i][j] - ratio[i][q] * square[j][q]
            for i in range(q + 1, GROUP):
                rows[i] = rows[i] - ratio[i][q] * rows[q]
            root = lax.rsqrt(pivot)
            root = root * (1.5 - 0.5 * pivot * root * root)
            scaled = rows[q] * root
            result = scaled if result is None else jnp.where(sub == q, scaled, result)
        done.append(jnp.where(lane <= sub + first, result, 0.0))
        if g + 1 < count:
            back = [None] * GROUP
            for q in reversed(range(GROUP)):
                back[q] = rows[q] * recip[q]
                for k in range(q + 1, GROUP):
                    back[q] = back[q] - ratio[k][q] * back[k]
            for i in range(g + 1, count):
                value = jnp.where(here, 0.0, groups[i])
                for q in range(GROUP):
                    value = value - cols[i - g][q] * back[q]
                groups[i] = value
    return jnp.concatenate(done, axis=0)


def inverse_factor_kernel(square_ref, inv_ref, row_ref):
    for owner in range(PIVOTS // SBLK):
        at = pivot_block(owner) * SBLK
        inv_ref[at : at + SBLK, :] = square_ref[owner * SBLK : (owner + 1) * SBLK, :]
    lane = lax.broadcasted_iota(jnp.int32, (TILE, TILE), 1)
    sub = lax.broadcasted_iota(jnp.int32, (TILE, TILE), 0)
    identity = jnp.where(lane == sub, 1.0, 0.0)
    steps = PIVOTS // TILE

    def step(k, carry):
        at = pl.ds(pl.multiple_of(k * TILE, TILE), TILE)
        inv_tile = inverse_factor_tile(inv_ref[at, at])
        inv_ref[at, at] = identity
        row_ref[...] = jnp.dot(
            inv_tile, inv_ref[at, :], precision=HIGHEST, preferred_element_type=jnp.float32
        )
        inv_ref[at, :] = row_ref[...]

        def below(i, carry):
            rows = pl.ds(pl.multiple_of(i * TILE, TILE), TILE)
            left = row_ref[:, rows]
            inv_ref[rows, at] = jnp.zeros((TILE, TILE), jnp.float32)
            inv_ref[rows, :] = inv_ref[rows, :] - lax.dot_general(
                left,
                row_ref[...],
                (((0,), (0,)), ((), ())),
                precision=HIGHEST,
                preferred_element_type=jnp.float32,
            )
            return carry

        return lax.fori_loop(k + 1, steps, below, carry)

    lax.fori_loop(0, steps, step, 0)
    for k in range(steps - 1):
        rows = slice(k * TILE, k * TILE + TILE)
        inv_ref[rows, (k + 1) * TILE :] = jnp.zeros((TILE, PIVOTS - (k + 1) * TILE), jnp.float32)


def inverse_factor(gathered):
    return pl.pallas_call(
        inverse_factor_kernel,
        grid=(1,),
        out_shape=jax.ShapeDtypeStruct((PIVOTS, PIVOTS), jnp.float32),
        in_specs=[pl.BlockSpec((PIVOTS, PIVOTS), lambda i: (0, 0))],
        out_specs=pl.BlockSpec((PIVOTS, PIVOTS), lambda i: (0, 0)),
        scratch_shapes=[pltpu.VMEM((TILE, PIVOTS), jnp.float32)],
        compiler_params=pltpu.CompilerParams(vmem_limit_bytes=56 << 20),
        cost_estimate=cost(70e-6, 8 << 20),
        name="inverse_factor",
    )(gathered)


def split(value):
    high = value.astype(jnp.bfloat16)
    return high, (value - high.astype(jnp.float32)).astype(jnp.bfloat16)


def keep_right(high_ref, low_ref, value, start, cols):
    high, low = split(value)
    for owner in range(PIVOTS // SBLK):
        at = pivot_block(owner) * SBLK - start
        if 0 <= at < value.shape[0]:
            rows = slice(owner * SBLK, (owner + 1) * SBLK)
            high_ref[rows, cols] = high[at : at + SBLK]
            low_ref[rows, cols] = low[at : at + SBLK]


def from_left(left, right):
    return lax.dot_general(
        left, right, (((0,), (0,)), ((), ())), preferred_element_type=jnp.float32
    )


def finish_kernel(
    place_ref, front_ref, left_ref, inv_ref, *refs
):
    above_refs, (out_ref, above_ref, solved_ref, high_ref, low_ref, sem) = refs[:-6], refs[-6:]
    slot = pl.program_id(0)
    row_index, col_index = place_ref[0], place_ref[1]
    trailing = col_index >= PANELS
    step = 256

    @pl.when((slot == 0) & trailing)
    def _():
        n_row = len(above_refs)
        away = (row_index + n_row - col_index % n_row) % n_row
        for index, source in enumerate(above_refs):

            @pl.when(away == index)
            def _():
                copies = []
                for owner in range(PIVOTS // SBLK):
                    at = pivot_block(owner) * SBLK
                    copies.append(
                        pltpu.make_async_copy(
                            source.at[owner * SBLK : (owner + 1) * SBLK, :],
                            above_ref.at[at : at + SBLK, :],
                            sem.at[owner],
                        )
                    )
                for copy in copies:
                    copy.start()
                for copy in copies:
                    copy.wait()

        for i in range(PIVOTS // step):
            rows = slice(i * step, (i + 1) * step)
            solved_ref[rows, :] = jnp.dot(
                inv_ref[rows, : (i + 1) * step],
                above_ref[: (i + 1) * step, :],
                precision=HIGHEST,
                preferred_element_type=jnp.float32,
            )
        for j in range(PIVOTS // step):
            rows = slice(j * step, (j + 1) * step)
            value = -lax.dot_general(
                inv_ref[j * step :, rows],
                solved_ref[j * step :, :],
                (((0,), (0,)), ((), ())),
                precision=HIGHEST,
                preferred_element_type=jnp.float32,
            )
            keep_right(high_ref, low_ref, value, j * step, slice(None))

    @pl.when((slot == 0) & jnp.logical_not(trailing))
    def _():
        for part in range(B // TILE):
            cols = slice(part * TILE, (part + 1) * TILE)
            own = pl.ds(pl.multiple_of(col_index * B + part * TILE, TILE), TILE)
            keep_right(high_ref, low_ref, inv_ref[own, :].T, 0, cols)

    left_high, left_low = split(left_ref[...])
    total = from_left(left_low, high_ref[...]) + from_left(left_high, low_ref[...])
    total = total + from_left(left_high, high_ref[...])
    out_ref[...] = total + jnp.where(trailing, front_ref[...], 0.0)

    @pl.when(slot == 0)
    def _():
        row = row_index * B + lax.broadcasted_iota(jnp.int32, (B, B), 0)
        col = col_index * B + lax.broadcasted_iota(jnp.int32, (B, B), 1)
        out_ref[...] = jnp.where((row < PIVOTS) & (row < col), 0.0, out_ref[...])


def finish(place, front, gathered, inverse, above):
    slots = front.shape[0] // B
    return pl.pallas_call(
        finish_kernel,
        grid=(slots,),
        out_shape=jax.ShapeDtypeStruct(front.shape, jnp.float32),
        in_specs=[
            smem_spec(),
            pl.BlockSpec((B, B), lambda s: (s, 0)),
            pl.BlockSpec((PIVOTS, B), lambda s: (0, s + PANELS)),
            vmem_spec(),
        ]
        + [pl.BlockSpec(memory_space=pl.ANY)] * len(above),
        out_specs=pl.BlockSpec((B, B), lambda s: (s, 0)),
        scratch_shapes=[
            pltpu.VMEM((PIVOTS, B), jnp.float32),
            pltpu.VMEM((PIVOTS, B), jnp.float32),
            pltpu.VMEM((PIVOTS, B), jnp.bfloat16),
            pltpu.VMEM((PIVOTS, B), jnp.bfloat16),
            pltpu.SemaphoreType.DMA((PIVOTS // SBLK,)),
        ],
        compiler_params=pltpu.CompilerParams(vmem_limit_bytes=40 << 20),
        cost_estimate=cost(22e-6, 26 << 20),
        name="finish",
    )(place, front, gathered, inverse, *above)


def land_kernel(target_ref, place_ref, part_ref, source_ref, out_ref):
    slot = pl.program_id(0)
    row_index, col_index = place_ref[0], place_ref[1]
    out_ref[...] = part_ref[...]

    @pl.when((col_index >= PANELS) & (slot * 4 + row_index >= PANELS))
    def _():
        for child in range(source_ref.shape[1] // SBLK):
            for t in range(source_ref.shape[0]):
                target = target_ref[child, t]

                @pl.when(target // (PER_PANEL * 4) == slot)
                def _():
                    rows = pl.ds(pl.multiple_of(target % PER_PANEL * SBLK, SBLK), SBLK)
                    at = slice(child * SBLK, (child + 1) * SBLK)
                    out_ref[rows, :] = out_ref[rows, :] + source_ref[t, at]


def land(targets, place, part, source):
    slots = part.shape[0] // B
    return pl.pallas_call(
        land_kernel,
        grid=(slots,),
        out_shape=jax.ShapeDtypeStruct(part.shape, jnp.float32),
        in_specs=[
            smem_spec(),
            smem_spec(),
            pl.BlockSpec((B, B), lambda s: (s, 0)),
            vmem_spec(),
        ],
        out_specs=pl.BlockSpec((B, B), lambda s: (s, 0)),
        input_output_aliases={2: 0},
        compiler_params=pltpu.CompilerParams(vmem_limit_bytes=16 << 20),
        cost_estimate=cost(5e-6, 12 << 20),
        name="land",
    )(targets, place, part, source)


def exchange(value):
    return lax.all_to_all(value, "col", split_axis=0, concat_axis=0, tiled=True)


def front_pieces(top, n_row, n_col, col_index):
    steps = B // SBLK
    received = []
    for step in range(steps):
        paths = []
        for panel in range(PANELS):
            for block in range(n_col):
                piece = (step + 2 * (block // n_row)) % steps
                paths.append((panel * n_col + block, block % n_row * n_col + piece * PANELS + panel))
        moved = []
        for slot in range(n_col // n_row):
            piece = (step + 2 * slot) % steps
            moved.append(top[piece * SBLK : (piece + 1) * SBLK])
        own_slot = col_index // n_row
        value = moved[0]
        for slot in range(1, n_col // n_row):
            value = jnp.where(own_slot == slot, moved[slot], value)
        received.append(lax.ppermute(value, ("row", "col"), paths))
    return received


def share_above(own, n_row, n_col):
    pieces = [own]
    for away in range(1, n_row):
        paths = []
        for col in range(n_col):
            root = col % n_row
            paths.append((root * n_col + col, (root + away) % n_row * n_col + col))
        pieces.append(lax.ppermute(own, ("row", "col"), paths))
    return pieces


def share_heads(own, n_row, row_index):
    moved = [own]
    for away in range(1, n_row):
        paths = [(row, (row + away) % n_row) for row in range(PANELS)]
        if away == n_row - 1:
            paths = [(0, n_row - 1), (1, 0)]
        moved.append(lax.ppermute(own, "row", paths))
    heads = []
    for panel in range(PANELS):
        value = moved[0]
        for away in range(1, n_row):
            value = jnp.where((row_index - panel) % n_row == away, moved[away], value)
        heads.append(value)
    return heads


def on_device(front_entries, child_updates, child_index, child_blocks):
    n_row = lax.axis_size("row")
    n_col = lax.axis_size("col")
    n_cube = lax.axis_size("cube")
    row_index = lax.axis_index("row")
    col_index = lax.axis_index("col")
    cube_index = lax.axis_index("cube")
    sibling = jnp.bitwise_xor(cube_index, 1)
    front = front_entries[0]
    own_block = row_index * n_col + col_index
    own_lists = child_index[cube_index]
    own_counts = child_blocks[cube_index]
    own_live = jnp.where(own_block < own_counts, own_counts, 0)
    block_lists = jnp.stack([own_lists[0], child_index[sibling, 1]])
    counts = jnp.stack([own_counts[0], child_blocks[sibling, 1]])
    live = jnp.where(own_block < counts, counts, 0)
    targets = lax.dynamic_slice(block_lists, (0, row_index * n_col), (2, n_col))
    place = jnp.stack([row_index, col_index])
    swap = [(cube, cube ^ 1) for cube in range(n_cube)]

    base = front_pieces(front[:B], n_row, n_col, col_index)
    picked_first, picked_second = pick(own_lists, own_live, child_updates[0])
    turned = exchange(turn(picked_first, picked_second))
    turned_second = lax.ppermute(turned[:, 1], "cube", swap)
    own_chunk = chunk(targets, place, base, turned[:, 0], turned_second, front.shape[0])
    heads = share_heads(own_chunk[:, :B], n_row, row_index)
    own_chunk = jnp.concatenate(heads + [own_chunk], axis=1)
    gathered = lax.all_gather(own_chunk, "col", axis=0, tiled=True)

    arrived_child = lax.ppermute(child_updates[0, 1], "cube", swap)
    spread = widen(block_lists, live, child_updates[0, 0], arrived_child)
    gathered, spread = lax.optimization_barrier((gathered, spread))
    arrived = exchange(spread)

    own_above = lax.dynamic_slice(
        gathered, (0, PIVOTS + col_index // n_row * B), (PIVOTS, B)
    )
    above = share_above(own_above, n_row, n_col)
    inverse = inverse_factor(gathered)
    part = finish(place, front, gathered, inverse, above)
    return land(targets, place, part, arrived)[None]


def solution(mesh):
    in_specs = (P("cube", "row", "col"), P("cube", None, ("row", "col"), None), P(), P())
    out_specs = P("cube", "row", "col")
    return jax.shard_map(
        on_device, mesh=mesh, in_specs=in_specs, out_specs=out_specs, check_vma=False
    )
```

```python
import jax
import jax.numpy as jnp
from jax import lax
from jax.experimental import pallas as pl
from jax.experimental.pallas import tpu as pltpu
from jax.sharding import PartitionSpec as P

F = 8192
B = 512
SBLK = 64
CR = 4096
PANELS = 2
PIVOTS = PANELS * B
PER_PANEL = B // SBLK
TILE = 128
GROUP = 8
HIGHEST = lax.Precision.HIGHEST
VMEM = pltpu.VMEM
SMEM = pltpu.SMEM


def vmem_spec():
    return pl.BlockSpec(memory_space=VMEM)


def smem_spec():
    return pl.BlockSpec(memory_space=SMEM)


def cost(seconds, moved):
    return pl.CostEstimate(flops=int(seconds * 1e15), bytes_accessed=moved, transcendentals=0)


def widen_kernel(list_ref, live_ref, first_ref, second_ref, out_ref):
    out_ref[...] = jnp.zeros_like(out_ref)
    lane = lax.broadcasted_iota(jnp.int32, (SBLK, TILE), 1)
    for child, rows_ref in enumerate((first_ref, second_ref)):
        out_rows = slice(child * SBLK, (child + 1) * SBLK)

        def place(pair, carry):
            both = rows_ref[:, pl.ds(pl.multiple_of(pair * TILE, TILE), TILE)]
            other = pltpu.roll(both, SBLK, 1)
            for half in range(2):
                block = pair * 2 + half
                target = list_ref[child, block]
                parity = target % 2
                offset = pl.multiple_of(target % PER_PANEL // 2 * TILE, TILE)
                owner = target // PER_PANEL
                moved = jnp.where(parity == half, both, other)
                keep = (lane // SBLK == parity) & (block < live_ref[child])
                spot = (owner, out_rows, pl.ds(offset, TILE))
                out_ref[spot] = jnp.where(keep, moved, out_ref[spot])
            return carry

        lax.fori_loop(0, CR // TILE, place, 0)


def widen(lists, live, first, second):
    return pl.pallas_call(
        widen_kernel,
        out_shape=jax.ShapeDtypeStruct((F // B, 2 * SBLK, B), jnp.float32),
        in_specs=[smem_spec(), smem_spec(), vmem_spec(), vmem_spec()],
        out_specs=vmem_spec(),
        compiler_params=pltpu.CompilerParams(vmem_limit_bytes=16 << 20),
        cost_estimate=cost(8e-6, 6 << 20),
        name="widen",
    )(lists, live, first, second)


def pivot_block(owner):
    return owner % PANELS * PER_PANEL + owner // PANELS


def pick_kernel(list_ref, live_ref, rows_ref, out_ref, picked_ref):
    half = SBLK // 2
    lane = lax.broadcasted_iota(jnp.int32, (SBLK, TILE), 1)
    for child in range(2):
        picked_ref[...] = jnp.zeros_like(picked_ref)
        for pair in range(rows_ref.shape[2] // TILE):
            both = rows_ref[child, :, pair * TILE : (pair + 1) * TILE]
            other = pltpu.roll(both, SBLK, 1)
            for part in range(2):
                block = pair * 2 + part
                target = list_ref[child, block]

                @pl.when((target < PANELS * PER_PANEL) & (block < live_ref[child]))
                def _():
                    parity = target % 2
                    moved = jnp.where(parity == part, both, other)
                    spot = pl.ds(pl.multiple_of(target // 2 * TILE, TILE), TILE)
                    picked_ref[:, spot] = jnp.where(
                        lane // SBLK == parity, moved, picked_ref[:, spot]
                    )

        turned = picked_ref[...].T
        for owner in range(out_ref.shape[0]):
            at = pivot_block(owner) * SBLK
            out_ref[owner, child] = jnp.concatenate(
                [turned[at : at + half], turned[at + half : at + SBLK]], axis=1
            )


def pick(lists, live, rows):
    width = PANELS * CR // 4
    owners = PIVOTS // SBLK
    shape = (owners, 2, SBLK // 2, 2 * SBLK)
    return pl.pallas_call(
        pick_kernel,
        grid=(1,),
        out_shape=jax.ShapeDtypeStruct(shape, jnp.float32),
        in_specs=[smem_spec(), smem_spec(), pl.BlockSpec((2, SBLK, width), lambda i: (0, 0, 0))],
        out_specs=pl.BlockSpec(shape, lambda i: (0, 0, 0, 0)),
        scratch_shapes=[pltpu.VMEM((SBLK, PIVOTS), jnp.float32)],
        compiler_params=pltpu.CompilerParams(vmem_limit_bytes=16 << 20),
        cost_estimate=cost(5e-6, 2 << 20),
        name="pick",
    )(lists, live, rows)


def chunk_kernel(target_ref, place_ref, *refs):
    base_refs, (first_ref, second_ref, out_ref, head_ref) = refs[:-4], refs[-4:]
    steps = len(base_refs)
    half = SBLK // 2
    own_piece = place_ref[1] // PANELS
    for slot in range(out_ref.shape[1] // B - PANELS):
        at = slice((slot + PANELS) * B, (slot + PANELS + 1) * B)
        for step in range(steps):

            @pl.when((step + 2 * slot) % steps == own_piece)
            def _():
                out_ref[:, at] = base_refs[step][...]

    lane = lax.broadcasted_iota(jnp.int32, (half, TILE), 1)
    for child, source in enumerate((first_ref, second_ref)):
        for t in range(source.shape[0]):
            both = source[t]
            other = pltpu.roll(both, SBLK, 1)
            target = target_ref[child, t]
            parity = target % 2
            slot = target // (PER_PANEL * 4) + PANELS
            offset = slot * B + target % PER_PANEL // 2 * TILE
            spot = pl.ds(pl.multiple_of(offset, TILE), TILE)
            keep = lane // SBLK == parity
            for part in range(2):
                rows = slice(part * half, (part + 1) * half)
                moved = jnp.where(parity == part, both, other)
                out_ref[rows, spot] = out_ref[rows, spot] + jnp.where(keep, moved, 0.0)
    head_ref[...] = out_ref[:, PANELS * B : (PANELS + 1) * B]
    out_ref[:, : PANELS * B] = jnp.zeros((SBLK, PANELS * B), jnp.float32)


def chunk(targets, place, base, first, second, width):
    return pl.pallas_call(
        chunk_kernel,
        out_shape=[
            jax.ShapeDtypeStruct((SBLK, PIVOTS + width), jnp.float32),
            jax.ShapeDtypeStruct((SBLK, B), jnp.float32),
        ],
        in_specs=[smem_spec(), smem_spec()] + [vmem_spec()] * (len(base) + 2),
        out_specs=[vmem_spec()] * 2,
        cost_estimate=cost(3e-6, 2 << 20),
        name="chunk",
    )(targets, place, *base, first, second)


def spread_over(value):
    return jnp.broadcast_to(value, (GROUP, TILE))


def inverse_factor_tile(tile):
    count = TILE // GROUP
    groups = [tile[GROUP * g : GROUP * g + GROUP, :] for g in range(count)]
    lane = lax.broadcasted_iota(jnp.int32, (GROUP, TILE), 1)
    sub = lax.broadcasted_iota(jnp.int32, (GROUP, TILE), 0)
    done = []
    for g in range(count):
        first = GROUP * g
        here = lane // GROUP == g
        own = groups[g]
        cols = [
            [spread_over(groups[i][:, first + q : first + q + 1]) for q in range(GROUP)]
            for i in range(g, count)
        ]
        square = [
            [spread_over(cols[0][q][i : i + 1, :]) if i >= q else None for q in range(GROUP)]
            for i in range(GROUP)
        ]
        rows = [
            jnp.where(here, jnp.where(lane == first + q, 1.0, 0.0), spread_over(own[q : q + 1, :]))
            for q in range(GROUP)
        ]
        ratio = [[None] * GROUP for _ in range(GROUP)]
        recip = [None] * GROUP
        result = None
        for q in range(GROUP):
            pivot = square[q][q]
            recip[q] = 1.0 / pivot
            for i in range(q + 1, GROUP):
                ratio[i][q] = square[i][q] * recip[q]
            for i in range(q + 1, GROUP):
                for j in range(q + 1, i + 1):
                    square[i][j] = square[i][j] - ratio[i][q] * square[j][q]
            for i in range(q + 1, GROUP):
                rows[i] = rows[i] - ratio[i][q] * rows[q]
            root = lax.rsqrt(pivot)
            root = root * (1.5 - 0.5 * pivot * root * root)
            scaled = rows[q] * root
            result = scaled if result is None else jnp.where(sub == q, scaled, result)
        done.append(jnp.where(lane <= sub + first, result, 0.0))
        if g + 1 < count:
            back = [None] * GROUP
            for q in reversed(range(GROUP)):
                back[q] = rows[q] * recip[q]
                for k in range(q + 1, GROUP):
                    back[q] = back[q] - ratio[k][q] * back[k]
            for i in range(g + 1, count):
                value = jnp.where(here, 0.0, groups[i])
                for q in range(GROUP):
                    value = value - cols[i - g][q] * back[q]
                groups[i] = value
    return jnp.concatenate(done, axis=0)


def split(value):
    high = value.astype(jnp.bfloat16)
    return high, (value - high.astype(jnp.float32)).astype(jnp.bfloat16)


def product(left, right, left_dim):
    def part(first, second):
        return lax.dot_general(
            first, second, (((left_dim,), (0,)), ((), ())), preferred_element_type=jnp.float32
        )

    return part(left[0], right[0]) + (part(left[1], right[0]) + part(left[0], right[1]))


def inverse_factor_kernel(
    square_ref, high_ref, low_ref, full_ref, row_ref, upper_high_ref, upper_low_ref
):
    for owner in range(PIVOTS // SBLK):
        at = pivot_block(owner) * SBLK
        full_ref[at : at + SBLK, :] = square_ref[owner * SBLK : (owner + 1) * SBLK, :]
    lane = lax.broadcasted_iota(jnp.int32, (TILE, PIVOTS), 1)
    steps = PIVOTS // TILE

    def step(k, carry):
        at = pl.ds(pl.multiple_of(k * TILE, TILE), TILE)

        @pl.when(k == 0)
        def _():
            row_ref[...] = full_ref[:TILE, :]

        for block in range(1, steps):

            @pl.when(k == block)
            def _():
                start = block * TILE
                own = slice(start, start + TILE)
                left = (upper_high_ref[:start, own], upper_low_ref[:start, own])
                right = (upper_high_ref[:start, start:], upper_low_ref[:start, start:])
                row_ref[:, start:] = full_ref[own, start:] - product(left, right, 0)
                right = (high_ref[:start, :start], low_ref[:start, :start])
                row_ref[:, :start] = -product(left, right, 0)

        tile = inverse_factor_tile(row_ref[:, at])
        row = product(split(tile), split(row_ref[...]), 1)
        upper_high_ref[at, :], upper_low_ref[at, :] = split(row)
        high_ref[at, :], low_ref[at, :] = split(jnp.where(lane < k * TILE, row, 0.0))
        high_ref[at, at], low_ref[at, at] = split(tile)
        return carry

    lax.fori_loop(0, steps, step, 0)


def inverse_factor(gathered):
    return pl.pallas_call(
        inverse_factor_kernel,
        grid=(1,),
        out_shape=[jax.ShapeDtypeStruct((PIVOTS, PIVOTS), jnp.bfloat16)] * 2,
        in_specs=[pl.BlockSpec((PIVOTS, PIVOTS), lambda i: (0, 0))],
        out_specs=[pl.BlockSpec((PIVOTS, PIVOTS), lambda i: (0, 0))] * 2,
        scratch_shapes=[
            pltpu.VMEM((PIVOTS, PIVOTS), jnp.float32),
            pltpu.VMEM((TILE, PIVOTS), jnp.float32),
            pltpu.VMEM((PIVOTS, PIVOTS), jnp.bfloat16),
            pltpu.VMEM((PIVOTS, PIVOTS), jnp.bfloat16),
        ],
        compiler_params=pltpu.CompilerParams(vmem_limit_bytes=48 << 20),
        cost_estimate=cost(65e-6, 8 << 20),
        name="inverse_factor",
    )(gathered)


def keep_right(high_ref, low_ref, value, start, cols):
    high, low = split(value)
    for owner in range(PIVOTS // SBLK):
        at = pivot_block(owner) * SBLK - start
        if 0 <= at < value.shape[0]:
            rows = slice(owner * SBLK, (owner + 1) * SBLK)
            high_ref[rows, cols] = high[at : at + SBLK]
            low_ref[rows, cols] = low[at : at + SBLK]


def finish_kernel(place_ref, front_ref, left_ref, inv_high_ref, inv_low_ref, *refs):
    above_refs = refs[:-7]
    out_ref, above_ref, solved_high_ref, solved_low_ref, high_ref, low_ref, sem = refs[-7:]
    slot = pl.program_id(0)
    row_index, col_index = place_ref[0], place_ref[1]
    trailing = col_index >= PANELS
    step = 256

    @pl.when((slot == 0) & trailing)
    def _():
        n_row = len(above_refs)
        away = (row_index + n_row - col_index % n_row) % n_row
        for index, source in enumerate(above_refs):

            @pl.when(away == index)
            def _():
                copies = []
                for owner in range(PIVOTS // SBLK):
                    at = pivot_block(owner) * SBLK
                    copies.append(
                        pltpu.make_async_copy(
                            source.at[owner * SBLK : (owner + 1) * SBLK, :],
                            above_ref.at[at : at + SBLK, :],
                            sem.at[owner],
                        )
                    )
                for copy in copies:
                    copy.start()
                for copy in copies:
                    copy.wait()

        above = split(above_ref[...])
        for i in range(PIVOTS // step):
            rows = slice(i * step, (i + 1) * step)
            end = (i + 1) * step
            left = (inv_high_ref[rows, :end], inv_low_ref[rows, :end])
            solved_high_ref[rows, :], solved_low_ref[rows, :] = split(
                product(left, (above[0][:end], above[1][:end]), 1)
            )
        for j in range(PIVOTS // step):
            rows = slice(j * step, (j + 1) * step)
            left = (inv_high_ref[j * step :, rows], inv_low_ref[j * step :, rows])
            right = (solved_high_ref[j * step :, :], solved_low_ref[j * step :, :])
            keep_right(high_ref, low_ref, -product(left, right, 0), j * step, slice(None))

    @pl.when((slot == 0) & jnp.logical_not(trailing))
    def _():
        for part in range(B // TILE):
            cols = slice(part * TILE, (part + 1) * TILE)
            own = pl.ds(pl.multiple_of(col_index * B + part * TILE, TILE), TILE)
            value = inv_high_ref[own, :].astype(jnp.float32) + inv_low_ref[own, :].astype(
                jnp.float32
            )
            keep_right(high_ref, low_ref, value.T, 0, cols)

    total = product(split(left_ref[...]), (high_ref[...], low_ref[...]), 0)
    out_ref[...] = total + jnp.where(trailing, front_ref[...], 0.0)

    @pl.when(slot == 0)
    def _():
        row = row_index * B + lax.broadcasted_iota(jnp.int32, (B, B), 0)
        col = col_index * B + lax.broadcasted_iota(jnp.int32, (B, B), 1)
        out_ref[...] = jnp.where((row < PIVOTS) & (row < col), 0.0, out_ref[...])


def finish(place, front, gathered, inverse, above):
    slots = front.shape[0] // B
    return pl.pallas_call(
        finish_kernel,
        grid=(slots,),
        out_shape=jax.ShapeDtypeStruct(front.shape, jnp.float32),
        in_specs=[
            smem_spec(),
            pl.BlockSpec((B, B), lambda s: (s, 0)),
            pl.BlockSpec((PIVOTS, B), lambda s: (0, s + PANELS)),
            vmem_spec(),
            vmem_spec(),
        ]
        + [pl.BlockSpec(memory_space=pl.ANY)] * len(above),
        out_specs=pl.BlockSpec((B, B), lambda s: (s, 0)),
        scratch_shapes=[pltpu.VMEM((PIVOTS, B), jnp.float32)]
        + [pltpu.VMEM((PIVOTS, B), jnp.bfloat16)] * 4
        + [pltpu.SemaphoreType.DMA((PIVOTS // SBLK,))],
        compiler_params=pltpu.CompilerParams(vmem_limit_bytes=30 << 20),
        cost_estimate=cost(16e-6, 26 << 20),
        name="finish",
    )(place, front, gathered, *inverse, *above)


def land_kernel(target_ref, place_ref, part_ref, source_ref, out_ref):
    slot = pl.program_id(0)
    row_index, col_index = place_ref[0], place_ref[1]
    out_ref[...] = part_ref[...]

    @pl.when((col_index >= PANELS) & (slot * 4 + row_index >= PANELS))
    def _():
        for child in range(source_ref.shape[1] // SBLK):
            for t in range(source_ref.shape[0]):
                target = target_ref[child, t]

                @pl.when(target // (PER_PANEL * 4) == slot)
                def _():
                    rows = pl.ds(pl.multiple_of(target % PER_PANEL * SBLK, SBLK), SBLK)
                    at = slice(child * SBLK, (child + 1) * SBLK)
                    out_ref[rows, :] = out_ref[rows, :] + source_ref[t, at]


def land(targets, place, part, source):
    slots = part.shape[0] // B
    return pl.pallas_call(
        land_kernel,
        grid=(slots,),
        out_shape=jax.ShapeDtypeStruct(part.shape, jnp.float32),
        in_specs=[
            smem_spec(),
            smem_spec(),
            pl.BlockSpec((B, B), lambda s: (s, 0)),
            vmem_spec(),
        ],
        out_specs=pl.BlockSpec((B, B), lambda s: (s, 0)),
        input_output_aliases={2: 0},
        compiler_params=pltpu.CompilerParams(vmem_limit_bytes=16 << 20),
        cost_estimate=cost(5e-6, 12 << 20),
        name="land",
    )(targets, place, part, source)


def exchange(value):
    return lax.all_to_all(value, "col", split_axis=0, concat_axis=0, tiled=True)


def front_pieces(top, n_row, n_col, col_index):
    steps = B // SBLK
    received = []
    for step in range(steps):
        paths = []
        for panel in range(PANELS):
            for block in range(n_col):
                piece = (step + 2 * (block // n_row)) % steps
                paths.append((panel * n_col + block, block % n_row * n_col + piece * PANELS + panel))
        moved = []
        for slot in range(n_col // n_row):
            piece = (step + 2 * slot) % steps
            moved.append(top[piece * SBLK : (piece + 1) * SBLK])
        own_slot = col_index // n_row
        value = moved[0]
        for slot in range(1, n_col // n_row):
            value = jnp.where(own_slot == slot, moved[slot], value)
        received.append(lax.ppermute(value, ("row", "col"), paths))
    return received


def share_above(own, n_row, n_col):
    pieces = [own]
    for away in range(1, n_row):
        paths = []
        for col in range(n_col):
            root = col % n_row
            paths.append((root * n_col + col, (root + away) % n_row * n_col + col))
        pieces.append(lax.ppermute(own, ("row", "col"), paths))
    return pieces


def share_heads(own, n_row, row_index):
    moved = [own]
    for away in range(1, n_row):
        paths = [(row, (row + away) % n_row) for row in range(PANELS)]
        if away == n_row - 1:
            paths = [(0, n_row - 1), (1, 0)]
        moved.append(lax.ppermute(own, "row", paths))
    heads = []
    for panel in range(PANELS):
        value = moved[0]
        for away in range(1, n_row):
            value = jnp.where((row_index - panel) % n_row == away, moved[away], value)
        heads.append(value)
    return heads


def on_device(front_entries, child_updates, child_index, child_blocks):
    n_row = lax.axis_size("row")
    n_col = lax.axis_size("col")
    n_cube = lax.axis_size("cube")
    row_index = lax.axis_index("row")
    col_index = lax.axis_index("col")
    cube_index = lax.axis_index("cube")
    sibling = jnp.bitwise_xor(cube_index, 1)
    front = front_entries[0]
    own_block = row_index * n_col + col_index
    own_lists = child_index[cube_index]
    own_counts = child_blocks[cube_index]
    own_live = jnp.where(own_block < own_counts, own_counts, 0)
    block_lists = jnp.stack([own_lists[0], child_index[sibling, 1]])
    counts = jnp.stack([own_counts[0], child_blocks[sibling, 1]])
    live = jnp.where(own_block < counts, counts, 0)
    targets = lax.dynamic_slice(block_lists, (0, row_index * n_col), (2, n_col))
    place = jnp.stack([row_index, col_index])
    swap = [(cube, cube ^ 1) for cube in range(n_cube)]

    base = front_pieces(front[:B], n_row, n_col, col_index)
    packed = pick(own_lists, own_live, child_updates[0])
    turned = exchange(packed)
    turned_second = lax.ppermute(turned[:, 1], "cube", swap)
    own_chunk, own_head = chunk(targets, place, base, turned[:, 0], turned_second, front.shape[0])
    heads = share_heads(own_head, n_row, row_index)
    for panel, head in enumerate(heads):
        own_chunk = lax.dynamic_update_slice(own_chunk, head, (0, panel * B))
    gathered = lax.all_gather(own_chunk, "col", axis=0, tiled=True)

    arrived_child = lax.ppermute(child_updates[0, 1], "cube", swap)
    spread = widen(block_lists, live, child_updates[0, 0], arrived_child)
    gathered, spread = lax.optimization_barrier((gathered, spread))
    arrived = exchange(spread)

    own_above = lax.dynamic_slice(
        gathered, (0, PIVOTS + col_index // n_row * B), (PIVOTS, B)
    )
    above = share_above(own_above, n_row, n_col)
    inverse = inverse_factor(gathered)
    part = finish(place, front, gathered, inverse, above)
    return land(targets, place, part, arrived)[None]


def solution(mesh):
    in_specs = (P("cube", "row", "col"), P("cube", None, ("row", "col"), None), P(), P())
    out_specs = P("cube", "row", "col")
    return jax.shard_map(
        on_device, mesh=mesh, in_specs=in_specs, out_specs=out_specs, check_vma=False
    )
```

```python
import functools

import jax
import jax.numpy as jnp
from jax import lax
from jax.experimental import pallas as pl
from jax.experimental.pallas import tpu as pltpu
from jax.sharding import PartitionSpec as P

F = 8192
B = 512
SBLK = 64
CR = 4096
PANELS = 2
PIVOTS = PANELS * B
PER_PANEL = B // SBLK
TILE = 128
GROUP = 8
HIGHEST = lax.Precision.HIGHEST
VMEM = pltpu.VMEM
SMEM = pltpu.SMEM


def vmem_spec():
    return pl.BlockSpec(memory_space=VMEM)


def smem_spec():
    return pl.BlockSpec(memory_space=SMEM)


def cost(seconds, moved):
    return pl.CostEstimate(flops=int(seconds * 1e15), bytes_accessed=moved, transcendentals=0)


def widen_kernel(parts, list_ref, live_ref, *refs):
    out_ref = refs[-1]
    out_ref[...] = jnp.zeros_like(out_ref)
    begin = 0
    for (child, start, count), rows_ref in zip(parts, refs[:-1]):
        lane = lax.broadcasted_iota(jnp.int32, (count, TILE), 1)
        in_rows = slice(start, start + count)
        out_rows = slice(begin, begin + count)
        begin += count

        def place(pair, carry):
            both = rows_ref[in_rows, pl.ds(pl.multiple_of(pair * TILE, TILE), TILE)]
            other = pltpu.roll(both, SBLK, 1)
            for half in range(2):
                block = pair * 2 + half
                target = list_ref[child, block]
                parity = target % 2
                offset = pl.multiple_of(target % PER_PANEL // 2 * TILE, TILE)
                owner = target // PER_PANEL
                moved = jnp.where(parity == half, both, other)
                keep = (lane // SBLK == parity) & (block < live_ref[child])
                spot = (owner, out_rows, pl.ds(offset, TILE))
                out_ref[spot] = jnp.where(keep, moved, out_ref[spot])
            return carry

        lax.fori_loop(0, CR // TILE, place, 0)


def widen(lists, live, parts, rows):
    total = sum(count for _, _, count in parts)
    return pl.pallas_call(
        functools.partial(widen_kernel, parts),
        out_shape=jax.ShapeDtypeStruct((F // B, total, B), jnp.float32),
        in_specs=[smem_spec(), smem_spec()] + [vmem_spec()] * len(rows),
        out_specs=vmem_spec(),
        compiler_params=pltpu.CompilerParams(vmem_limit_bytes=16 << 20),
        cost_estimate=cost(total * 6e-8, total * 50000),
        name="widen",
    )(lists, live, *rows)


def pivot_block(owner):
    return owner % PANELS * PER_PANEL + owner // PANELS


def pick_kernel(list_ref, live_ref, rows_ref, out_ref, picked_ref):
    half = SBLK // 2
    lane = lax.broadcasted_iota(jnp.int32, (SBLK, TILE), 1)
    for child in range(2):
        picked_ref[...] = jnp.zeros_like(picked_ref)
        for pair in range(rows_ref.shape[2] // TILE):
            both = rows_ref[child, :, pair * TILE : (pair + 1) * TILE]
            other = pltpu.roll(both, SBLK, 1)
            for part in range(2):
                block = pair * 2 + part
                target = list_ref[child, block]

                @pl.when((target < PANELS * PER_PANEL) & (block < live_ref[child]))
                def _():
                    parity = target % 2
                    moved = jnp.where(parity == part, both, other)
                    spot = pl.ds(pl.multiple_of(target // 2 * TILE, TILE), TILE)
                    picked_ref[:, spot] = jnp.where(
                        lane // SBLK == parity, moved, picked_ref[:, spot]
                    )

        turned = picked_ref[...].T
        for owner in range(out_ref.shape[0]):
            at = pivot_block(owner) * SBLK
            out_ref[owner, child] = jnp.concatenate(
                [turned[at : at + half], turned[at + half : at + SBLK]], axis=1
            )


def pick(lists, live, rows):
    width = PANELS * CR // 4
    owners = PIVOTS // SBLK
    shape = (owners, 2, SBLK // 2, 2 * SBLK)
    return pl.pallas_call(
        pick_kernel,
        grid=(1,),
        out_shape=jax.ShapeDtypeStruct(shape, jnp.float32),
        in_specs=[smem_spec(), smem_spec(), pl.BlockSpec((2, SBLK, width), lambda i: (0, 0, 0))],
        out_specs=pl.BlockSpec(shape, lambda i: (0, 0, 0, 0)),
        scratch_shapes=[pltpu.VMEM((SBLK, PIVOTS), jnp.float32)],
        compiler_params=pltpu.CompilerParams(vmem_limit_bytes=16 << 20),
        cost_estimate=cost(5e-6, 2 << 20),
        name="pick",
    )(lists, live, rows)


def chunk_kernel(target_ref, place_ref, *refs):
    base_refs, (first_ref, second_ref, out_ref, head_ref) = refs[:-4], refs[-4:]
    steps = len(base_refs)
    half = SBLK // 2
    own_piece = place_ref[1] // PANELS
    for slot in range(out_ref.shape[1] // B - PANELS):
        at = slice((slot + PANELS) * B, (slot + PANELS + 1) * B)
        for step in range(steps):

            @pl.when((step + 2 * slot) % steps == own_piece)
            def _():
                out_ref[:, at] = base_refs[step][...]

    lane = lax.broadcasted_iota(jnp.int32, (half, TILE), 1)
    for child, source in enumerate((first_ref, second_ref)):
        for t in range(source.shape[0]):
            both = source[t]
            other = pltpu.roll(both, SBLK, 1)
            target = target_ref[child, t]
            parity = target % 2
            slot = target // (PER_PANEL * 4) + PANELS
            offset = slot * B + target % PER_PANEL // 2 * TILE
            spot = pl.ds(pl.multiple_of(offset, TILE), TILE)
            keep = lane // SBLK == parity
            for part in range(2):
                rows = slice(part * half, (part + 1) * half)
                moved = jnp.where(parity == part, both, other)
                out_ref[rows, spot] = out_ref[rows, spot] + jnp.where(keep, moved, 0.0)
    head_ref[...] = out_ref[:, PANELS * B : (PANELS + 1) * B]
    out_ref[:, : PANELS * B] = jnp.zeros((SBLK, PANELS * B), jnp.float32)


def chunk(targets, place, base, first, second, width):
    return pl.pallas_call(
        chunk_kernel,
        out_shape=[
            jax.ShapeDtypeStruct((SBLK, PIVOTS + width), jnp.float32),
            jax.ShapeDtypeStruct((SBLK, B), jnp.float32),
        ],
        in_specs=[smem_spec(), smem_spec()] + [vmem_spec()] * (len(base) + 2),
        out_specs=[vmem_spec()] * 2,
        cost_estimate=cost(3e-6, 2 << 20),
        name="chunk",
    )(targets, place, *base, first, second)


def spread_over(value):
    return jnp.broadcast_to(value, (GROUP, TILE))


def inverse_factor_tile(tile):
    count = TILE // GROUP
    groups = [tile[GROUP * g : GROUP * g + GROUP, :] for g in range(count)]
    lane = lax.broadcasted_iota(jnp.int32, (GROUP, TILE), 1)
    sub = lax.broadcasted_iota(jnp.int32, (GROUP, TILE), 0)
    done = []
    for g in range(count):
        first = GROUP * g
        here = lane // GROUP == g
        own = groups[g]
        cols = [
            [spread_over(groups[i][:, first + q : first + q + 1]) for q in range(GROUP)]
            for i in range(g, count)
        ]
        square = [
            [spread_over(cols[0][q][i : i + 1, :]) if i >= q else None for q in range(GROUP)]
            for i in range(GROUP)
        ]
        rows = [
            jnp.where(here, jnp.where(lane == first + q, 1.0, 0.0), spread_over(own[q : q + 1, :]))
            for q in range(GROUP)
        ]
        ratio = [[None] * GROUP for _ in range(GROUP)]
        recip = [None] * GROUP
        result = None
        for q in range(GROUP):
            pivot = square[q][q]
            recip[q] = 1.0 / pivot
            for i in range(q + 1, GROUP):
                ratio[i][q] = square[i][q] * recip[q]
            for i in range(q + 1, GROUP):
                for j in range(q + 1, i + 1):
                    square[i][j] = square[i][j] - ratio[i][q] * square[j][q]
            for i in range(q + 1, GROUP):
                rows[i] = rows[i] - ratio[i][q] * rows[q]
            root = lax.rsqrt(pivot)
            root = root * (1.5 - 0.5 * pivot * root * root)
            scaled = rows[q] * root
            result = scaled if result is None else jnp.where(sub == q, scaled, result)
        done.append(jnp.where(lane <= sub + first, result, 0.0))
        if g + 1 < count:
            back = [None] * GROUP
            for q in reversed(range(GROUP)):
                back[q] = rows[q] * recip[q]
                for k in range(q + 1, GROUP):
                    back[q] = back[q] - ratio[k][q] * back[k]
            for i in range(g + 1, count):
                value = jnp.where(here, 0.0, groups[i])
                for q in range(GROUP):
                    value = value - cols[i - g][q] * back[q]
                groups[i] = value
    return jnp.concatenate(done, axis=0)


def split(value):
    high = value.astype(jnp.bfloat16)
    return high, (value - high.astype(jnp.float32)).astype(jnp.bfloat16)


def product(left, right, left_dim):
    def part(first, second):
        return lax.dot_general(
            first, second, (((left_dim,), (0,)), ((), ())), preferred_element_type=jnp.float32
        )

    return part(left[0], right[0]) + (part(left[1], right[0]) + part(left[0], right[1]))


def inverse_factor_kernel(
    square_ref, high_ref, low_ref, full_ref, row_ref, upper_high_ref, upper_low_ref
):
    for owner in range(PIVOTS // SBLK):
        at = pivot_block(owner) * SBLK
        full_ref[at : at + SBLK, :] = square_ref[owner * SBLK : (owner + 1) * SBLK, :]
    lane = lax.broadcasted_iota(jnp.int32, (TILE, PIVOTS), 1)
    steps = PIVOTS // TILE

    def step(k, carry):
        at = pl.ds(pl.multiple_of(k * TILE, TILE), TILE)

        @pl.when(k == 0)
        def _():
            row_ref[...] = full_ref[:TILE, :]

        for block in range(1, steps):

            @pl.when(k == block)
            def _():
                start = block * TILE
                own = slice(start, start + TILE)
                left = (upper_high_ref[:start, own], upper_low_ref[:start, own])
                right = (upper_high_ref[:start, start:], upper_low_ref[:start, start:])
                row_ref[:, start:] = full_ref[own, start:] - product(left, right, 0)
                right = (high_ref[:start, :start], low_ref[:start, :start])
                row_ref[:, :start] = -product(left, right, 0)

        tile = inverse_factor_tile(row_ref[:, at])
        row = product(split(tile), split(row_ref[...]), 1)
        upper_high_ref[at, :], upper_low_ref[at, :] = split(row)
        high_ref[at, :], low_ref[at, :] = split(jnp.where(lane < k * TILE, row, 0.0))
        high_ref[at, at], low_ref[at, at] = split(tile)
        return carry

    lax.fori_loop(0, steps, step, 0)


def inverse_factor(gathered):
    return pl.pallas_call(
        inverse_factor_kernel,
        grid=(1,),
        out_shape=[jax.ShapeDtypeStruct((PIVOTS, PIVOTS), jnp.bfloat16)] * 2,
        in_specs=[pl.BlockSpec((PIVOTS, PIVOTS), lambda i: (0, 0))],
        out_specs=[pl.BlockSpec((PIVOTS, PIVOTS), lambda i: (0, 0))] * 2,
        scratch_shapes=[
            pltpu.VMEM((PIVOTS, PIVOTS), jnp.float32),
            pltpu.VMEM((TILE, PIVOTS), jnp.float32),
            pltpu.VMEM((PIVOTS, PIVOTS), jnp.bfloat16),
            pltpu.VMEM((PIVOTS, PIVOTS), jnp.bfloat16),
        ],
        compiler_params=pltpu.CompilerParams(vmem_limit_bytes=48 << 20),
        cost_estimate=cost(65e-6, 8 << 20),
        name="inverse_factor",
    )(gathered)


def keep_right(high_ref, low_ref, value, start, cols):
    high, low = split(value)
    for owner in range(PIVOTS // SBLK):
        at = pivot_block(owner) * SBLK - start
        if 0 <= at < value.shape[0]:
            rows = slice(owner * SBLK, (owner + 1) * SBLK)
            high_ref[rows, cols] = high[at : at + SBLK]
            low_ref[rows, cols] = low[at : at + SBLK]


def finish_kernel(place_ref, front_ref, left_ref, inv_high_ref, inv_low_ref, *refs):
    above_refs = refs[:-7]
    out_ref, above_ref, solved_high_ref, solved_low_ref, high_ref, low_ref, sem = refs[-7:]
    slot = pl.program_id(0)
    row_index, col_index = place_ref[0], place_ref[1]
    trailing = col_index >= PANELS
    step = 256

    @pl.when((slot == 0) & trailing)
    def _():
        n_row = len(above_refs)
        away = (row_index + n_row - col_index % n_row) % n_row
        for index, source in enumerate(above_refs):

            @pl.when(away == index)
            def _():
                copies = []
                for owner in range(PIVOTS // SBLK):
                    at = pivot_block(owner) * SBLK
                    copies.append(
                        pltpu.make_async_copy(
                            source.at[owner * SBLK : (owner + 1) * SBLK, :],
                            above_ref.at[at : at + SBLK, :],
                            sem.at[owner],
                        )
                    )
                for copy in copies:
                    copy.start()
                for copy in copies:
                    copy.wait()

        above = split(above_ref[...])
        for i in range(PIVOTS // step):
            rows = slice(i * step, (i + 1) * step)
            end = (i + 1) * step
            left = (inv_high_ref[rows, :end], inv_low_ref[rows, :end])
            solved_high_ref[rows, :], solved_low_ref[rows, :] = split(
                product(left, (above[0][:end], above[1][:end]), 1)
            )
        for j in range(PIVOTS // step):
            rows = slice(j * step, (j + 1) * step)
            left = (inv_high_ref[j * step :, rows], inv_low_ref[j * step :, rows])
            right = (solved_high_ref[j * step :, :], solved_low_ref[j * step :, :])
            keep_right(high_ref, low_ref, -product(left, right, 0), j * step, slice(None))

    @pl.when((slot == 0) & jnp.logical_not(trailing))
    def _():
        for part in range(B // TILE):
            cols = slice(part * TILE, (part + 1) * TILE)
            own = pl.ds(pl.multiple_of(col_index * B + part * TILE, TILE), TILE)
            value = inv_high_ref[own, :].astype(jnp.float32) + inv_low_ref[own, :].astype(
                jnp.float32
            )
            keep_right(high_ref, low_ref, value.T, 0, cols)

    total = product(split(left_ref[...]), (high_ref[...], low_ref[...]), 0)
    out_ref[...] = total + jnp.where(trailing, front_ref[...], 0.0)

    @pl.when(slot == 0)
    def _():
        row = row_index * B + lax.broadcasted_iota(jnp.int32, (B, B), 0)
        col = col_index * B + lax.broadcasted_iota(jnp.int32, (B, B), 1)
        out_ref[...] = jnp.where((row < PIVOTS) & (row < col), 0.0, out_ref[...])


def finish(place, front, gathered, inverse, above):
    slots = front.shape[0] // B
    return pl.pallas_call(
        finish_kernel,
        grid=(slots,),
        out_shape=jax.ShapeDtypeStruct(front.shape, jnp.float32),
        in_specs=[
            smem_spec(),
            pl.BlockSpec((B, B), lambda s: (s, 0)),
            pl.BlockSpec((PIVOTS, B), lambda s: (0, s + PANELS)),
            vmem_spec(),
            vmem_spec(),
        ]
        + [pl.BlockSpec(memory_space=pl.ANY)] * len(above),
        out_specs=pl.BlockSpec((B, B), lambda s: (s, 0)),
        scratch_shapes=[pltpu.VMEM((PIVOTS, B), jnp.float32)]
        + [pltpu.VMEM((PIVOTS, B), jnp.bfloat16)] * 4
        + [pltpu.SemaphoreType.DMA((PIVOTS // SBLK,))],
        compiler_params=pltpu.CompilerParams(vmem_limit_bytes=30 << 20),
        cost_estimate=cost(16e-6, 26 << 20),
        name="finish",
    )(place, front, gathered, *inverse, *above)


def land_kernel(target_ref, place_ref, part_ref, early_ref, late_ref, out_ref):
    slot = pl.program_id(0)
    row_index, col_index = place_ref[0], place_ref[1]
    early = early_ref.shape[1]
    out_ref[...] = part_ref[...]

    @pl.when((col_index >= PANELS) & (slot * 4 + row_index >= PANELS))
    def _():
        for child in range(2):
            for t in range(late_ref.shape[0]):
                target = target_ref[child, t]

                @pl.when(target // (PER_PANEL * 4) == slot)
                def _():
                    begin = target % PER_PANEL * SBLK
                    if child == 0:
                        rows = pl.ds(pl.multiple_of(begin, SBLK), early)
                        out_ref[rows, :] = out_ref[rows, :] + early_ref[t]
                        rows = pl.ds(pl.multiple_of(begin + early, 8), SBLK - early)
                        out_ref[rows, :] = out_ref[rows, :] + late_ref[t, : SBLK - early]
                    else:
                        rows = pl.ds(pl.multiple_of(begin, SBLK), SBLK)
                        out_ref[rows, :] = out_ref[rows, :] + late_ref[t, SBLK - early :]


def land(targets, place, part, early, late):
    slots = part.shape[0] // B
    return pl.pallas_call(
        land_kernel,
        grid=(slots,),
        out_shape=jax.ShapeDtypeStruct(part.shape, jnp.float32),
        in_specs=[
            smem_spec(),
            smem_spec(),
            pl.BlockSpec((B, B), lambda s: (s, 0)),
            vmem_spec(),
            vmem_spec(),
        ],
        out_specs=pl.BlockSpec((B, B), lambda s: (s, 0)),
        input_output_aliases={2: 0},
        compiler_params=pltpu.CompilerParams(vmem_limit_bytes=16 << 20),
        cost_estimate=cost(5e-6, 12 << 20),
        name="land",
    )(targets, place, part, early, late)


def exchange(value):
    return lax.all_to_all(value, "col", split_axis=0, concat_axis=0, tiled=True)


def front_pieces(top, n_row, n_col, col_index):
    steps = B // SBLK
    received = []
    for step in range(steps):
        paths = []
        for panel in range(PANELS):
            for block in range(n_col):
                piece = (step + 2 * (block // n_row)) % steps
                paths.append((panel * n_col + block, block % n_row * n_col + piece * PANELS + panel))
        moved = []
        for slot in range(n_col // n_row):
            piece = (step + 2 * slot) % steps
            moved.append(top[piece * SBLK : (piece + 1) * SBLK])
        own_slot = col_index // n_row
        value = moved[0]
        for slot in range(1, n_col // n_row):
            value = jnp.where(own_slot == slot, moved[slot], value)
        received.append(lax.ppermute(value, ("row", "col"), paths))
    return received


def share_above(own, n_row, n_col):
    pieces = [own]
    for away in range(1, n_row):
        paths = []
        for col in range(n_col):
            root = col % n_row
            paths.append((root * n_col + col, (root + away) % n_row * n_col + col))
        pieces.append(lax.ppermute(own, ("row", "col"), paths))
    return pieces


def share_heads(own, n_row, row_index):
    moved = [own]
    for away in range(1, n_row):
        paths = [(row, (row + away) % n_row) for row in range(PANELS)]
        if away == n_row - 1:
            paths = [(0, n_row - 1), (1, 0)]
        moved.append(lax.ppermute(own, "row", paths))
    heads = []
    for panel in range(PANELS):
        value = moved[0]
        for away in range(1, n_row):
            value = jnp.where((row_index - panel) % n_row == away, moved[away], value)
        heads.append(value)
    return heads


def on_device(front_entries, child_updates, child_index, child_blocks):
    n_row = lax.axis_size("row")
    n_col = lax.axis_size("col")
    n_cube = lax.axis_size("cube")
    row_index = lax.axis_index("row")
    col_index = lax.axis_index("col")
    cube_index = lax.axis_index("cube")
    sibling = jnp.bitwise_xor(cube_index, 1)
    front = front_entries[0]
    own_block = row_index * n_col + col_index
    own_lists = child_index[cube_index]
    own_counts = child_blocks[cube_index]
    own_live = jnp.where(own_block < own_counts, own_counts, 0)
    block_lists = jnp.stack([own_lists[0], child_index[sibling, 1]])
    counts = jnp.stack([own_counts[0], child_blocks[sibling, 1]])
    live = jnp.where(own_block < counts, counts, 0)
    targets = lax.dynamic_slice(block_lists, (0, row_index * n_col), (2, n_col))
    place = jnp.stack([row_index, col_index])
    swap = [(cube, cube ^ 1) for cube in range(n_cube)]

    base = front_pieces(front[:B], n_row, n_col, col_index)
    packed = pick(own_lists, own_live, child_updates[0])
    turned = exchange(packed)
    turned_second = lax.ppermute(turned[:, 1], "cube", swap)
    own_chunk, own_head = chunk(targets, place, base, turned[:, 0], turned_second, front.shape[0])
    early = SBLK // 2
    own_rows = child_updates[0, 0]
    spread_early = widen(block_lists, live, ((0, 0, early),), (own_rows,))
    own_head, spread_early = lax.optimization_barrier((own_head, spread_early))
    heads = share_heads(own_head, n_row, row_index)
    arrived_early = exchange(spread_early)
    for panel, head in enumerate(heads):
        own_chunk = lax.dynamic_update_slice(own_chunk, head, (0, panel * B))
    gathered = lax.all_gather(own_chunk, "col", axis=0, tiled=True)

    arrived_child = lax.ppermute(child_updates[0, 1], "cube", swap)
    parts = ((0, early, SBLK - early), (1, 0, SBLK))
    spread = widen(block_lists, live, parts, (own_rows, arrived_child))
    gathered, spread = lax.optimization_barrier((gathered, spread))
    arrived = exchange(spread)

    own_above = lax.dynamic_slice(
        gathered, (0, PIVOTS + col_index // n_row * B), (PIVOTS, B)
    )
    above = share_above(own_above, n_row, n_col)
    inverse = inverse_factor(gathered)
    part = finish(place, front, gathered, inverse, above)
    return land(targets, place, part, arrived_early, arrived)[None]


def solution(mesh):
    in_specs = (P("cube", "row", "col"), P("cube", None, ("row", "col"), None), P(), P())
    out_specs = P("cube", "row", "col")
    return jax.shard_map(
        on_device, mesh=mesh, in_specs=in_specs, out_specs=out_specs, check_vma=False
    )
```
